256 devices in a mesh: dp: 16 (over z, core), tensor: 16 (over x, y).
Axes of the slice: x: 4, y: 4, z: 8, core: 2. Of those that a mesh axis runs over, the one named last changes fastest.
Arguments:
- queries: bfloat16 [2048, 8192], P('dp', 'tensor'), parts along dimension 0
- tree_states: bfloat16 [2048, 2048], P(('dp', 'tensor')), parts along dimension 0, may hold values from -6 to 6
- cache_codes: bfloat16 [5120, 8, 2, 64, 128], P(('dp', 'tensor')), parts along dimension 0, may hold values from 0 to 255, as said below
- cache_scales: float32 [5120, 8, 2, 128], P(('dp', 'tensor')), parts along dimension 0, may hold values from 0.3 to 3
- bit_widths: int32 [128], P('dp'), parts along dimension 0, may hold values from 2 to 8, as said below
- page_table: int32 [64, 80], P('dp'), parts along dimension 0, may hold values from 0 to 19, as said below
- lengths: int32 [64], P('dp'), parts along dimension 0, may hold values from 1 to 5120, as said below
- parents: int32 [64, 32], P('dp'), parts along dimension 0, may hold values from 0 to 30, as said below
- tree_mask: int32 [64, 32, 32], P('dp'), parts along dimension 0, may hold values from 0 to 1, as said below
- output_weight: bfloat16 [8192, 8192], P('tensor'), may hold values from -0.09375 to 0.09375
- residual: bfloat16 [2048, 8192], P('dp', 'tensor'), parts along dimension 0
- norm_gain: bfloat16 [8192], P('tensor'), may hold values from 0.099609375 to 1.8984375
- draft_weight: bfloat16 [8192, 2048], P('tensor'), may hold values from -0.09375 to 0.09375
Outputs:
- feature: bfloat16 [2048, 8192], P('dp', 'tensor'), parts along dimension 0
- draft_projection: bfloat16 [2048, 2048], P('dp', 'tensor'), parts along dimension 0
The draws below stay inside these ranges and needn't reach their ends.
There are 16 independent parts, one for each index of `dp`. The reference program is written for one: setup_inputs(seed, part) draws one part's arguments, and reference() takes and returns one part's arrays. A program takes and returns all parts, laid end to end along the dimension named above; an argument that names none is the same for every part. Nothing has to cross between parts.
Inputs may be any that keep to these rules, and one draw needn't show every extreme that they name: `bit_widths`: every head holds 2, 4 or 8 bits. `cache_codes`: on KV head g every entry is a whole number from 0 to 2 to the power bit_widths[g], minus 1. `page_table`: for each c, the entries of columns c * 5 to (c + 1) * 5 - 1 over all requests form a permutation of 0 to 19: slots in the pool of tensor index c. `lengths`: some request of every part has exactly 5120 positions. parents[r, 0] = 0; for i > 0 the parent is below i, in node i's own block of 8 nodes, or in the first block when i is the first node of its block. tree_mask[r, i, j] = 1 exactly when j is i or an ancestor of i under parents.
All inputs are finite; a program needn't handle non-finite values.
Results may differ from the reference program's by a relative error of at most 0.012.
Values may be sent and summed in bfloat16 or wider, within the bound.
No kernel may reach another device: no remote copies, remote signals or barrier semaphores. Data moves between devices by JAX's collectives and lax.ppermute only.
A program may use at most 128 MiB of HBM per device.

```python
import math
import jax
import jax.numpy as jnp
import numpy as np
from jax import lax

D = 8192
HQ = 64
KVH = 8
HD = 128
NODES = 32
TBLOCK = 8
PAGE = 64
PAGES_DEV = 5
REQS = 4
CTX = 5120
POOL = 20
ROWS = 128
N_TENSOR = 16


def bit_helper(key, part):
    combos = 3 ** KVH
    offset = jax.random.randint(jax.random.fold_in(key, 11), (), 0, combos, dtype=jnp.int32)
    number = (offset + jnp.asarray(part, jnp.int32)) % combos
    powers = jnp.asarray(np.power(3, np.arange(KVH)).astype(np.int32))
    digits = number // powers % 3
    return jnp.left_shift(jnp.int32(2), digits.astype(jnp.int32)).astype(jnp.int32)


def draw_bit_widths(key, part):
    return bit_helper(key, part)


def draw_cache_codes(key, part):
    widths = bit_helper(key, part)
    ceiling = jnp.left_shift(jnp.int32(1), widths)[None, :, None, None, None]
    levels_drawn = jax.random.randint(jax.random.fold_in(key, 12), (N_TENSOR * POOL, KVH, 2, PAGE, HD), 0, ceiling, dtype=jnp.int32)
    return levels_drawn.astype(jnp.float32).astype(jnp.bfloat16)


def one_permutation(device_key):
    return jax.random.permutation(device_key, POOL)


def draw_page_table(key, part):
    device_keys = jax.random.split(jax.random.fold_in(key, 21), N_TENSOR)
    shuffled = jax.vmap(one_permutation)(device_keys)
    arranged = shuffled.reshape(N_TENSOR, REQS, PAGES_DEV).transpose(1, 0, 2)
    return arranged.reshape(REQS, N_TENSOR * PAGES_DEV).astype(jnp.int32)


def draw_lengths(key, part):
    drawn = jax.random.randint(jax.random.fold_in(key, 31), (REQS,), 1, CTX + 1, dtype=jnp.int32)
    chosen = jax.random.randint(jax.random.fold_in(key, 32), (), 0, REQS, dtype=jnp.int32)
    return jnp.where(jnp.arange(REQS, dtype=jnp.int32) == chosen, CTX, drawn).astype(jnp.int32)


def tree_helper(key):
    node_ids = jnp.arange(NODES, dtype=jnp.int32)
    block_first = node_ids % TBLOCK == 0
    lowest = jnp.where(block_first, 0, node_ids // TBLOCK * TBLOCK)
    highest = jnp.where(node_ids == 0, 1, jnp.where(block_first, TBLOCK, node_ids))
    parent = jax.random.randint(jax.random.fold_in(key, 41), (REQS, NODES), lowest[None, :], highest[None, :], dtype=jnp.int32)
    parent = jnp.where(node_ids[None, :] == 0, 0, parent).astype(jnp.int32)
    last_node = (node_ids[None, :] == NODES - 1) & (jnp.arange(REQS, dtype=jnp.int32)[:, None] == 0)
    parent = jnp.where(last_node, NODES - 2, parent).astype(jnp.int32)

    def closure(parent_row):

        def add_node(lineage_rows, node):
            ancestors = jnp.where(node > 0, lineage_rows[parent_row[node]], jnp.zeros((NODES,), jnp.int32))
            lineage = jnp.maximum(ancestors, (node_ids == node).astype(jnp.int32))
            return (lineage_rows.at[node].set(lineage), None)
        result, unused = lax.scan(add_node, jnp.zeros((NODES, NODES), jnp.int32), node_ids)
        return result
    return (parent, jax.vmap(closure)(parent))


def draw_parents(key, part):
    parent, lineage = tree_helper(key)
    return parent


def draw_tree_mask(key, part):
    parent, lineage = tree_helper(key)
    return lineage.astype(jnp.int32)


def draw_queries(key, part):
    sample_key = jax.random.fold_in(jax.random.fold_in(key, 61), 0)
    sample = 2.0 * jax.random.normal(sample_key, (ROWS, HQ, HD), jnp.float32)
    return sample.reshape(ROWS, HQ * HD).astype(jnp.bfloat16)


def draw_residual(key, part):
    sample_key, column_key, row_key = jax.random.split(jax.random.fold_in(key, 51), 3)
    rising = jnp.exp(jnp.log(3.0) * (jnp.arange(D, dtype=jnp.float32) / D - 0.5))
    column_scale = jnp.exp(jax.random.uniform(column_key, (D,), jnp.float32, jnp.log(0.5), jnp.log(2.0)))
    row_scale = jnp.exp(jax.random.uniform(row_key, (ROWS, 1), jnp.float32, jnp.log(0.3), jnp.log(3.0)))
    sample = jax.random.normal(sample_key, (ROWS, D), jnp.float32)
    return (sample * rising[None, :] * column_scale[None, :] * row_scale).astype(jnp.bfloat16)


def with_spikes(array, rng, source, target, parts, factor):
    owner, partner = [(jnp.arange(array.shape[axis_at]) // (array.shape[axis_at] // parts)).reshape([-1 if axis == axis_at else 1 for axis in range(array.ndim)]) for axis_at in (source, target)]
    chosen = jax.random.permutation(rng, parts)[partner]
    strong = (owner == chosen) | (owner == (partner + parts // 2) % parts)
    return jnp.where(strong, factor * array, array)


def shard_levels(key, dims, cuts, smallest, largest):
    loudness, own = 1.0, jax.random.fold_in(key, 6)
    for axis_at, shards_of in cuts:
        heights = jnp.exp(jax.random.uniform(jax.random.fold_in(own, axis_at), (shards_of,), jnp.float32, smallest / len(cuts), largest / len(cuts)))
        loudness = loudness * jnp.repeat(heights, dims[axis_at] // shards_of).reshape([-1 if axis == axis_at else 1 for axis in range(len(dims))])
    return loudness


def noise(rng, dims, deviation, most, shards=(), held_as=jnp.bfloat16):
    entries = jax.random.normal(rng, dims, jnp.float32) * deviation
    if len(shards) > 0:
        entries = shard_levels(rng, dims, shards, -0.22, 0.18) * entries
    return jnp.clip(entries, min=-most, max=most).astype(held_as)


def heavy_noise(rng, extent, deviation, bound, cuts, heavy, kind=jnp.bfloat16):
    values = deviation * jax.random.normal(rng, extent, jnp.float32)
    if cuts:
        values = values * shard_levels(rng, extent, cuts, -0.22, 0.18)
    return jnp.clip(with_spikes(values, jax.random.fold_in(rng, 3), *heavy), -bound, bound).astype(kind)


def setup_inputs(seed: int = 0, part: int = 0) -> dict:
    key_list = jax.random.split(jax.random.key(seed), 14)
    part_splits = jax.random.split(jax.random.fold_in(key_list[13], part), 14)
    return {
        "queries": draw_queries(jax.random.fold_in(jax.random.fold_in(key_list[13], part), 71), part),
        "tree_states": noise(part_splits[1], (ROWS, 2 * KVH * HD), 1.0, 6.0, ((0, 16),)),
        "cache_codes": draw_cache_codes(jax.random.fold_in(jax.random.fold_in(key_list[13], part), 71), part),
        "cache_scales": jnp.clip(jnp.exp(math.log(3.0) - 2.3025851 * jax.random.uniform(part_splits[3], (N_TENSOR * POOL, KVH, 2, HD), jnp.float32) ** shard_levels(part_splits[3], (N_TENSOR * POOL, KVH, 2, HD), ((0, 16),), -0.2, 0.2)), 0.3, 3.0),
        "bit_widths": draw_bit_widths(jax.random.fold_in(jax.random.fold_in(key_list[13], part), 71), part),
        "page_table": draw_page_table(jax.random.fold_in(jax.random.fold_in(key_list[13], part), 71), part),
        "lengths": draw_lengths(jax.random.fold_in(jax.random.fold_in(key_list[13], part), 71), part),
        "parents": draw_parents(jax.random.fold_in(jax.random.fold_in(key_list[13], part), 71), part),
        "tree_mask": draw_tree_mask(jax.random.fold_in(jax.random.fold_in(key_list[13], part), 71), part),
        "output_weight": heavy_noise(key_list[9], (HQ * HD, D), (HQ * HD) ** -0.5, 0.09375, ((0, 16),), (0, 1, 16, 2.0)),
        "residual": draw_residual(jax.random.fold_in(jax.random.fold_in(key_list[13], part), 71), part),
        "norm_gain": jnp.clip(1.0 + 0.18 * jax.random.normal(key_list[11], (D,), jnp.float32), 0.099609375, 1.8984375).astype(jnp.bfloat16),
        "draft_weight": heavy_noise(key_list[12], (D, 2 * KVH * HD), D ** -0.5, 0.09375, ((0, 16),), (0, 1, 16, 2.0)),
    }


masked_score = -1e+30
epsilon = 1e-05

def rounded(values):
    return lax.optimization_barrier(values.astype(jnp.bfloat16)).astype(jnp.float32)

def dequantize(cache_codes, cache_scales, bit_widths):
    levels = jnp.exp2(bit_widths.astype(jnp.float32))[None, :, None, None, None]
    drawn = cache_codes.astype(jnp.float32)
    scaled = cache_scales.astype(jnp.float32)[:, :, :, None, :]
    return (scaled * (2.0 * drawn - levels + 1.0) / levels).astype(jnp.bfloat16)

def block_partial(request_query, key_rows, value_rows, in_range):
    scores = jnp.einsum('nkgd,ktd->nkgt', request_query, key_rows.astype(jnp.float32)) / math.sqrt(HD)
    live = in_range[None, None, None, :]
    scores = jnp.where(live, scores, masked_score)
    block_max = lax.optimization_barrier(jnp.max(scores, axis=-1))
    weights = jnp.where(live, jnp.exp(scores - block_max[..., None]), 0.0)
    block_sum = lax.optimization_barrier(jnp.sum(weights, axis=-1))
    block_out = jnp.einsum('nkgt,ktd->nkgd', rounded(weights), value_rows.astype(jnp.float32))
    block_out = block_out / jnp.where(block_sum > 0, block_sum, 1.0)[..., None]
    return (block_max, block_sum, block_out.astype(jnp.bfloat16))

def reference(queries, tree_states, cache_codes, cache_scales, bit_widths, page_table, lengths, parents, tree_mask, output_weight, residual, norm_gain, draft_weight):
    groups = HQ // KVH
    block_span = PAGES_DEV * PAGE
    dequant = dequantize(cache_codes, cache_scales, bit_widths)
    tree_keys = tree_states[:, :KVH * HD].reshape(REQS, NODES, KVH, HD).astype(jnp.float32)
    tree_values = tree_states[:, KVH * HD:].reshape(REQS, NODES, KVH, HD).astype(jnp.float32)
    outputs = []
    for request in range(REQS):
        request_query = queries[request * NODES:(request + 1) * NODES].astype(jnp.float32).reshape(NODES, KVH, groups, HD)
        request_pages = page_table[request]
        request_length = lengths[request]

        def one_block(block_id):
            slot_ids = block_id * POOL + lax.dynamic_slice_in_dim(request_pages, block_id * PAGES_DEV, PAGES_DEV)
            chosen = jnp.take(dequant, slot_ids, axis=0)
            key_rows = chosen[:, :, 0].transpose(1, 0, 2, 3).reshape(KVH, block_span, HD)
            value_rows = chosen[:, :, 1].transpose(1, 0, 2, 3).reshape(KVH, block_span, HD)
            positions = block_id * block_span + jnp.arange(block_span, dtype=jnp.int32)
            return block_partial(request_query, key_rows, value_rows, positions < request_length)
        maxima, sums, partial_out = lax.map(one_block, jnp.arange(N_TENSOR, dtype=jnp.int32))
        allowed = (tree_mask[request] > 0)[:, None, None, :]
        tree_scores = jnp.einsum('nkgd,jkd->nkgj', request_query, tree_keys[request]) / math.sqrt(HD)
        tree_scores = jnp.where(allowed, tree_scores, masked_score)
        overall = jnp.maximum(lax.optimization_barrier(jnp.max(maxima, axis=0)), lax.optimization_barrier(jnp.max(tree_scores, axis=-1)))
        rescale = jnp.exp(maxima - overall[None]) * sums
        numerator = lax.optimization_barrier(jnp.sum(rescale[..., None] * partial_out.astype(jnp.float32), axis=0))
        denominator = lax.optimization_barrier(jnp.sum(rescale, axis=0))
        tree_weights = jnp.where(allowed, jnp.exp(tree_scores - overall[..., None]), 0.0)
        numerator = numerator + jnp.einsum('nkgj,jkd->nkgd', rounded(tree_weights), tree_values[request])
        denominator = denominator + lax.optimization_barrier(jnp.sum(tree_weights, axis=-1))
        attended = (numerator / denominator[..., None]).astype(jnp.bfloat16)
        outputs.append(attended.reshape(NODES, HQ * HD))
    attended = jnp.concatenate(outputs, axis=0)
    projected = jnp.dot(attended, output_weight, preferred_element_type=jnp.float32)
    feature = (residual.astype(jnp.float32) + projected).astype(jnp.bfloat16)
    squares = lax.optimization_barrier(jnp.sum(jnp.square(feature.astype(jnp.float32)), axis=1))
    inverse = lax.rsqrt(squares / D + epsilon)
    normed = (feature.astype(jnp.float32) * inverse[:, None] * norm_gain.astype(jnp.float32)[None, :]).astype(jnp.bfloat16)
    row_ids = (jnp.arange(REQS, dtype=jnp.int32)[:, None] * NODES + parents).reshape(ROWS).astype(jnp.int32)
    chosen_rows = jnp.take(normed, row_ids, axis=0)
    draft_projection = jnp.dot(chosen_rows, draft_weight, preferred_element_type=jnp.float32).astype(jnp.bfloat16)
    return (feature, draft_projection)
```

```python
import math

import jax
import jax.numpy as jnp
from jax import lax
from jax.experimental import pallas as pl
from jax.experimental.pallas import tpu as pltpu
from jax.sharding import PartitionSpec as P

D = 8192
HQ = 64
KVH = 8
HD = 128
NODES = 32
PAGE = 64
PAGES_DEV = 5
REQS = 4
ROWS = 128
N_TENSOR = 16
SPAN = PAGES_DEV * PAGE
GROUPS = HQ // KVH
HEADS = HQ // N_TENSOR
QCOLS = HEADS * HD

masked_score = -1e30
epsilon = 1e-05
SCALE = math.log2(math.e) / math.sqrt(HD)

OUT_ROWS = REQS * HD
LSE_AT = OUT_ROWS
TREE_AT = OUT_ROWS + 16
XROWS = OUT_ROWS + 32

bf16 = jnp.bfloat16
f32 = jnp.float32


def dot(a, b, dims):
    return lax.dot_general(a, b, (dims, ((), ())), preferred_element_type=f32)


def split3(x):
    hi = x.astype(bf16)
    rest = x - hi.astype(f32)
    mid = rest.astype(bf16)
    lo = (rest - mid.astype(f32)).astype(bf16)
    return hi, mid, lo


def dequant_body(table, place, bits, *refs):
    codes = refs[:PAGES_DEV]
    scales = refs[PAGES_DEV : 2 * PAGES_DEV]
    keys, values = refs[2 * PAGES_DEV :]
    for g in range(KVH):
        levels = lax.shift_left(jnp.int32(1), bits[g]).astype(f32)
        inverse = 1.0 / jnp.full((1, HD), levels, f32)
        parts = []
        for p in range(PAGES_DEV):
            scaled = scales[p][0, g] * inverse
            drawn = codes[p][0, g].astype(f32)
            centred = 2.0 * drawn - (levels - 1.0)
            keys[0, g, p * PAGE : (p + 1) * PAGE, :] = (centred[0] * scaled[0:1]).astype(bf16)
            parts.append(centred[1] * scaled[1:2])
        values[0, g] = jnp.concatenate(parts, axis=0).T.astype(bf16)


def dequantize(codes, scales, bits, table, place):
    def code_spec(p):
        return pl.BlockSpec(
            (1, KVH, 2, PAGE, HD),
            lambda r, table, place, bits: (table[r, place[0] * PAGES_DEV + p], 0, 0, 0, 0),
        )

    def scale_spec(p):
        return pl.BlockSpec(
            (1, KVH, 2, HD),
            lambda r, table, place, bits: (table[r, place[0] * PAGES_DEV + p], 0, 0, 0),
        )

    pages = range(PAGES_DEV)
    return pl.pallas_call(
        dequant_body,
        grid_spec=pltpu.PrefetchScalarGridSpec(
            num_scalar_prefetch=3,
            grid=(REQS,),
            in_specs=[code_spec(p) for p in pages] + [scale_spec(p) for p in pages],
            out_specs=[
                pl.BlockSpec((1, KVH, SPAN, HD), lambda r, *_: (r, 0, 0, 0)),
                pl.BlockSpec((1, KVH, HD, SPAN), lambda r, *_: (r, 0, 0, 0)),
            ],
        ),
        out_shape=[
            jax.ShapeDtypeStruct((REQS, KVH, SPAN, HD), bf16),
            jax.ShapeDtypeStruct((REQS, KVH, HD, SPAN), bf16),
        ],
        cost_estimate=pl.CostEstimate(
            flops=20_000_000, bytes_accessed=2 * codes.size * 2, transcendentals=0
        ),
        name="dequantize",
    )(table, place, bits, *([codes] * PAGES_DEV), *([scales] * PAGES_DEV))


def block_body(place, lengths, queries, keys, values, tree, out, lse):
    r = pl.program_id(0)
    live_count = lengths[r] - place[0] * SPAN
    live = lax.broadcasted_iota(jnp.int32, (SPAN, 1), 0) < live_count
    for g in range(KVH):
        query = jnp.concatenate(
            [
                queries[2 * g + h // HEADS, :, (h % HEADS) * HD : (h % HEADS + 1) * HD]
                for h in range(GROUPS)
            ],
            axis=0,
        )
        scores = dot(keys[0, g], query, ((1,), (1,)))
        scores = jnp.where(live, scores, masked_score)
        largest = jnp.max(scores, axis=0, keepdims=True)
        weights = jnp.exp2((scores - largest) * SCALE)
        total = jnp.sum(weights, axis=0, keepdims=True)
        mixed = dot(values[0, g], weights.astype(bf16), ((1,), (0,))) * (1.0 / total)
        mixed = mixed.astype(bf16)
        block_lse = jnp.where(live_count > 0, largest * SCALE + jnp.log2(total), masked_score)
        for half in range(2):
            lanes = slice(half * HD, (half + 1) * HD)
            out[2 * g + half, pl.ds(pl.multiple_of(r * HD, HD), HD), :] = mixed[:, lanes]
            lse[2 * g + half, pl.ds(r, 1), :] = block_lse[:, lanes]

    @pl.when(r == REQS - 1)
    def _():
        for t in range(N_TENSOR):
            pieces = split3(lse[t, 0:REQS, :])
            out[t, LSE_AT : LSE_AT + 16, :] = jnp.concatenate(
                [p.astype(f32) for p in pieces] + [jnp.zeros((4, HD), f32)], axis=0
            ).astype(bf16)
            g = t // 2
            out[t, TREE_AT : TREE_AT + 16, :] = jnp.concatenate(
                [
                    tree[:, g * HD : (g + 1) * HD].astype(f32),
                    tree[:, (KVH + g) * HD : (KVH + g + 1) * HD].astype(f32),
                ],
                axis=0,
            ).astype(bf16)


def block_partial(place, lengths, queries, keys, values, tree):
    return pl.pallas_call(
        block_body,
        grid_spec=pltpu.PrefetchScalarGridSpec(
            num_scalar_prefetch=2,
            grid=(REQS,),
            in_specs=[
                pl.BlockSpec((N_TENSOR, NODES, QCOLS), lambda r, *_: (0, r, 0)),
                pl.BlockSpec((1, KVH, SPAN, HD), lambda r, *_: (r, 0, 0, 0)),
                pl.BlockSpec((1, KVH, HD, SPAN), lambda r, *_: (r, 0, 0, 0)),
                pl.BlockSpec((8, 2 * KVH * HD), lambda r, *_: (0, 0)),
            ],
            out_specs=pl.BlockSpec((N_TENSOR, XROWS, HD), lambda r, *_: (0, 0, 0)),
            scratch_shapes=[pltpu.VMEM((N_TENSOR, 8, HD), f32)],
        ),
        out_shape=jax.ShapeDtypeStruct((N_TENSOR, XROWS, HD), bf16),
        cost_estimate=pl.CostEstimate(
            flops=1_400_000_000, bytes_accessed=10_000_000, transcendentals=2_600_000
        ),
        name="block_partial",
    )(place, lengths, queries, keys, values, tree)


WCOLS = 1024
WBLOCKS = D // WCOLS


def combine_body(parts, query, mask, weight, out, held, attended, sems):
    def fetch(b):
        return pltpu.make_async_copy(
            weight.at[:, b * WCOLS : (b + 1) * WCOLS], held.at[b], sems.at[b]
        )

    for b in range(WBLOCKS):
        fetch(b).start()
    lses = []
    for t in range(N_TENSOR):
        rows = parts[t, LSE_AT : LSE_AT + 16, :].astype(f32)
        lses.append(rows[0:4] + rows[4:8] + rows[8:12])
    for r in range(REQS):
        own = jnp.concatenate(
            [
                query[r * NODES : (r + 1) * NODES, h * HD : (h + 1) * HD]
                for h in range(HEADS)
            ],
            axis=0,
        )
        tree_keys = jnp.concatenate(
            [parts[4 * r + k, TREE_AT : TREE_AT + 8, :] for k in range(4)], axis=0
        )
        tree_values = jnp.concatenate(
            [parts[4 * r + k, TREE_AT + 8 : TREE_AT + 16, :] for k in range(4)], axis=0
        )
        allowed = mask[r] > 0
        scores = dot(tree_keys, own, ((1,), (1,))) * SCALE
        scores = jnp.where(allowed, scores, masked_score)
        overall = jnp.max(scores, axis=0, keepdims=True)
        for t in range(N_TENSOR):
            overall = jnp.maximum(overall, lses[t][r : r + 1])
        tree_weights = jnp.where(allowed, jnp.exp2(scores - overall), 0.0)
        denominator = jnp.sum(tree_weights, axis=0, keepdims=True)
        numerator = dot(tree_values, tree_weights.astype(bf16), ((0,), (0,)))
        for t in range(N_TENSOR):
            share = jnp.exp2(lses[t][r : r + 1] - overall)
            denominator = denominator + share
            numerator = numerator + share * parts[t, r * HD : (r + 1) * HD, :].astype(f32)
        mixed = (numerator * (1.0 / denominator)).T.astype(bf16)
        for h in range(HEADS):
            attended[r * NODES : (r + 1) * NODES, h * HD : (h + 1) * HD] = mixed[
                h * NODES : (h + 1) * NODES
            ]
    for b in range(WBLOCKS):
        fetch(b).wait()
        product = dot(attended[...], held[b], ((1,), (0,))).astype(bf16)
        out[2 * b] = product[:, :QCOLS]
        out[2 * b + 1] = product[:, QCOLS:]


def combine_project(parts, query, mask, weight):
    vmem = pl.BlockSpec(memory_space=pltpu.VMEM)
    return pl.pallas_call(
        combine_body,
        in_specs=[vmem, vmem, vmem, pl.BlockSpec(memory_space=pl.ANY)],
        out_specs=vmem,
        out_shape=jax.ShapeDtypeStruct((N_TENSOR, ROWS, QCOLS), bf16),
        scratch_shapes=[
            pltpu.VMEM((WBLOCKS, QCOLS, WCOLS), bf16),
            pltpu.VMEM((ROWS, QCOLS), bf16),
            pltpu.SemaphoreType.DMA((WBLOCKS,)),
        ],
        cost_estimate=pl.CostEstimate(
            flops=1_100_000_000, bytes_accessed=13_000_000, transcendentals=40_000
        ),
        name="combine_project",
    )(parts, query, mask, weight)


def draft_body(parts, residual, gain, chooser, weight, feature, out):
    total = residual[...].astype(f32)
    summed = parts[0].astype(f32)
    for t in range(1, N_TENSOR):
        summed = summed + parts[t].astype(f32)
    rounded = (total + summed).astype(bf16)
    feature[...] = rounded
    wide = rounded.astype(f32)
    squares = jnp.sum(wide * wide, axis=1, keepdims=True)
    eye = lax.broadcasted_iota(jnp.int32, (ROWS, ROWS), 0) == lax.broadcasted_iota(
        jnp.int32, (ROWS, ROWS), 1
    )
    squares_row = jnp.sum(jnp.where(eye, squares, 0.0), axis=0, keepdims=True)
    hi, mid, lo = split3(squares_row)
    pieces = jnp.concatenate(
        [hi.astype(f32), mid.astype(f32), lo.astype(f32), jnp.zeros((5, ROWS), f32)], axis=0
    ).astype(bf16)
    gained = (wide * gain[...].astype(f32)).astype(bf16)
    chosen = dot(chooser[...], gained, ((1,), (0,))).astype(bf16)
    product = dot(chosen, weight[...], ((1,), (0,))).astype(bf16)
    for t in range(N_TENSOR):
        out[t, 0:ROWS, :] = product[:, t * HD : (t + 1) * HD]
        out[t, ROWS : ROWS + 8, :] = pieces


def draft(parts, residual, gain, chooser, weight):
    vmem = pl.BlockSpec(memory_space=pltpu.VMEM)
    return pl.pallas_call(
        draft_body,
        in_specs=[vmem] * 5,
        out_specs=[vmem, vmem],
        out_shape=[
            jax.ShapeDtypeStruct((ROWS, QCOLS), bf16),
            jax.ShapeDtypeStruct((N_TENSOR, ROWS + 8, HD), bf16),
        ],
        cost_estimate=pl.CostEstimate(
            flops=300_000_000, bytes_accessed=5_000_000, transcendentals=0
        ),
        name="draft",
    )(parts, residual, gain, chooser, weight)


def finish_body(parts, chooser, out):
    summed = parts[0].astype(f32)
    for t in range(1, N_TENSOR):
        summed = summed + parts[t].astype(f32)
    squares = summed[ROWS : ROWS + 1] + summed[ROWS + 1 : ROWS + 2] + summed[ROWS + 2 : ROWS + 3]
    inverse = lax.rsqrt(squares / D + epsilon)
    column = jnp.sum(chooser[...].astype(f32) * inverse, axis=1, keepdims=True)
    out[...] = (summed[0:ROWS] * column).astype(bf16)


def finish(parts, chooser):
    vmem = pl.BlockSpec(memory_space=pltpu.VMEM)
    return pl.pallas_call(
        finish_body,
        in_specs=[vmem, vmem],
        out_specs=vmem,
        out_shape=jax.ShapeDtypeStruct((ROWS, HD), bf16),
        cost_estimate=pl.CostEstimate(flops=1_000_000, bytes_accessed=700_000, transcendentals=128),
        name="finish",
    )(parts, chooser)


def exchange(x):
    return lax.all_to_all(x, "tensor", 0, 0)


def shards(
    queries,
    tree_states,
    cache_codes,
    cache_scales,
    bit_widths,
    page_table,
    lengths,
    parents,
    tree_mask,
    output_weight,
    residual,
    norm_gain,
    draft_weight,
):
    place = lax.axis_index("tensor").astype(jnp.int32).reshape(1)
    every_query = exchange(jnp.broadcast_to(queries[None], (N_TENSOR, ROWS, QCOLS)))
    keys, values = dequantize(cache_codes, cache_scales, bit_widths, page_table, place)
    mask = jnp.tile(tree_mask.transpose(0, 2, 1), (1, 1, HEADS)).astype(f32)
    row_ids = (jnp.arange(REQS, dtype=jnp.int32)[:, None] * NODES + parents).reshape(ROWS)
    chooser = (row_ids[:, None] == jnp.arange(ROWS, dtype=jnp.int32)[None, :]).astype(bf16)
    parts = exchange(block_partial(place, lengths, every_query, keys, values, tree_states))
    products = exchange(combine_project(parts, queries, mask, output_weight))
    feature, drafted = draft(products, residual, norm_gain[None, :], chooser, draft_weight)
    return (feature, finish(exchange(drafted), chooser))


def solution(mesh):
    placed = (
        P("dp", "tensor"),
        P(("dp", "tensor"), None),
        P(("dp", "tensor"), None, None, None, None),
        P(("dp", "tensor"), None, None, None),
        P("dp"),
        P("dp", None),
        P("dp"),
        P("dp", None),
        P("dp", None, None),
        P("tensor", None),
        P("dp", "tensor"),
        P("tensor"),
        P("tensor", None),
    )
    return jax.shard_map(
        shards,
        mesh=mesh,
        in_specs=placed,
        out_specs=(P("dp", "tensor"), P("dp", "tensor")),
        check_vma=False,
    )
```
